32 devices in a mesh: dp: 2 (over x), ctx: 16 (over z, y, core).
Axes of the slice: x: 2, y: 2, z: 4, core: 2. Of those that a mesh axis runs over, the one named last changes fastest.
Arguments:
- hidden: bfloat16 [16384, 4096], P(('dp', 'ctx')), parts along dimension 0, may hold values from -24 to 24
- dest: int32 [16384], P(('dp', 'ctx')), parts along dimension 0, may hold values from 0 to 8191, as said below
- doc_ids: int32 [16384], P('dp'), parts along dimension 0, may hold values from 0 to 63, never falling along the last dimension, each value on 1 to 1024 neighbouring positions
- w_query: bfloat16 [4096, 2048], P('ctx'), may hold values from -0.09375 to 0.09375
- key_weight: bfloat16 [4096, 512], P('ctx'), may hold values from -0.09375 to 0.09375
- value_weight: bfloat16 [4096, 512], P('ctx'), may hold values from -0.09375 to 0.09375
Outputs:
- attended: bfloat16 [16384, 2048], P(('dp', 'ctx')), parts along dimension 0
The draws below stay inside these ranges and needn't reach their ends.
There are 2 independent parts, one for each index of `dp`. The reference program is written for one: setup_inputs(seed, part) draws one part's arguments, and reference() takes and returns one part's arrays. A program takes and returns all parts, laid end to end along the dimension named above; an argument that names none is the same for every part. Nothing has to cross between parts.
Inputs may be any that keep to these rules, and one draw needn't show every extreme that they name: `dest`: A permutation. Each block of 512 loader rows sends at most 64 rows to one block of 512 context positions, exactly 64 to some.
All inputs are finite; a program needn't handle non-finite values.
Results may differ from the reference program's by a relative error of at most 0.024.
Values may be sent and summed in bfloat16 or wider, within the bound.
No kernel may reach another device: no remote copies, remote signals or barrier semaphores. Data moves between devices by JAX's collectives and lax.ppermute only.
A program may use at most 128 MiB of HBM per device.

```python
import math
import jax
import jax.numpy as jnp
import numpy as np
from jax import lax

MODEL_WIDTH = 4096
QUERY_HEADS = 16
KEY_VALUE_HEADS = 4
HEAD_SIZE = 128
BLOCK_TOKENS = 512
SEQ = 8192
DOCS = 64
N_CTX = 16


def draw_hidden(key, part):
    values_drawn = jnp.clip(jax.random.normal(key, (SEQ, MODEL_WIDTH), jnp.float32), -4.0, 4.0)
    return values_drawn.astype(jnp.bfloat16)


def draw_dest(key, part):
    cycle_size = N_CTX
    rows_dev = BLOCK_TOKENS
    capacity = 2 * rows_dev // cycle_size
    shift_key = jax.random.fold_in(key, 11)
    source_key = jax.random.fold_in(key, 13)
    target_key = jax.random.fold_in(key, 17)
    shifts = jax.random.permutation(shift_key, cycle_size)
    piece_count = 3 * cycle_size // 4
    counts = jnp.where(jnp.arange(piece_count) < cycle_size // 4, capacity, capacity // 2)
    piece_ends = jnp.cumsum(counts)
    slots = jnp.arange(rows_dev, dtype=jnp.int32)
    piece_of = jnp.sum((slots[:, None] >= piece_ends[None, :]).astype(jnp.int32), axis=1)
    shift_of = shifts[piece_of]
    sigma = jax.vmap(lambda sub_key: jax.random.permutation(sub_key, rows_dev))(jax.random.split(source_key, cycle_size))
    tau_table = jax.vmap(lambda sub_key: jax.random.permutation(sub_key, rows_dev))(jax.random.split(target_key, cycle_size))
    sources = jnp.arange(cycle_size, dtype=jnp.int32)[:, None]
    owners = (sources + shift_of[None, :]) % cycle_size
    loader = sources * rows_dev + sigma
    target = owners * rows_dev + tau_table[owners, slots[None, :]]
    result = jnp.zeros((SEQ,), jnp.int32).at[loader.reshape(-1)].set(target.reshape(-1).astype(jnp.int32))
    return result


def levels(stream_key, dims, shards, low, high):
    def one(dim, parts):
        heights = jax.random.uniform(jax.random.fold_in(jax.random.fold_in(stream_key, 6), dim), (parts,), jnp.float32, low / len(shards), high / len(shards))
        return jnp.repeat(jnp.exp(heights), dims[dim] // parts).reshape((-1,) + (1,) * (len(dims) - dim - 1))

    level = one(*shards[0])
    for cut in shards[1:]:
        level = level * one(*cut)
    return level


def profile(amount, total, most, slope):
    weights = [(1 << 20) // math.isqrt(rank ** slope) + 1 for rank in range(2, amount + 1)]
    spare, given = total - most - (amount - 1), [1] * (amount - 1)
    while spare > 0:
        movable = [i for i in range(amount - 1) if given[i] < most]
        mass, left = sum([weights[i] for i in movable]), spare
        for i in movable:
            more = min(most - given[i], max(1, left * weights[i] // mass), spare)
            given[i] = given[i] + more
            spare = spare - more
    return np.array([most] + given)


def uneven_parts(rng, number_of, total, bound, slope):
    if number_of == 2:
        one = jax.random.randint(rng, (), max(1, total - bound), min(bound, total - 1) + 1)
        return jnp.stack([one, total - one])
    sizes = jnp.asarray(profile(number_of, total, bound, slope), jnp.int32)
    couples = (number_of - 1) // 2
    source_of, taker = sizes[1:1 + 2 * couples:2], sizes[2:2 + 2 * couples:2]
    slack = jnp.minimum(source_of - 1, bound - taker)
    shifted = jax.random.randint(jax.random.fold_in(rng, 1), (couples,), 0, 1 << 20) % (slack + 1)
    sizes = sizes.at[1:1 + 2 * couples:2].set(source_of - shifted).at[2:2 + 2 * couples:2].set(taker + shifted)
    return sizes[jax.random.permutation(jax.random.fold_in(rng, 2), number_of)]


def noise(key, extent, scale, most, cuts=(), kind=jnp.bfloat16):
    drawn = scale * jax.random.normal(key, extent, jnp.float32)
    if cuts:
        drawn = drawn * levels(key, extent, cuts, -0.22, 0.18)
    return jnp.clip(drawn, -most, most).astype(kind)


def setup_inputs(seed: int = 0, part: int = 0) -> dict:
    arg_keys = jax.random.split(jax.random.key(seed), 7)
    own_keys = jax.random.split(jax.random.fold_in(arg_keys[6], part), 7)
    return {
        "hidden": draw_hidden(jax.random.fold_in(jax.random.fold_in(arg_keys[6], part), 71), part),
        "dest": draw_dest(jax.random.fold_in(jax.random.fold_in(arg_keys[6], part), 71), part),
        "doc_ids": jnp.searchsorted(jnp.cumsum(uneven_parts(own_keys[2], DOCS, SEQ, 2 * BLOCK_TOKENS, 2)), jnp.arange(SEQ), side="right").astype(jnp.int32),
        "w_query": noise(arg_keys[3], (MODEL_WIDTH, QUERY_HEADS * HEAD_SIZE), MODEL_WIDTH ** -0.5, 0.09375, ((0, 16),)),
        "key_weight": noise(arg_keys[4], (MODEL_WIDTH, KEY_VALUE_HEADS * HEAD_SIZE), MODEL_WIDTH ** -0.5, 0.09375, ((0, 16),)),
        "value_weight": noise(arg_keys[5], (MODEL_WIDTH, KEY_VALUE_HEADS * HEAD_SIZE), MODEL_WIDTH ** -0.5, 0.09375, ((0, 16),)),
    }


rope_base = 500000.0 * 16.0 ** (128.0 / 126.0)
masked_score = -1.0e30


def apply_rotation(values, token_positions, head_count):
    head_width = values.shape[-1] // head_count
    half_width = head_width // 2
    freq_index = jnp.arange(half_width, dtype=jnp.float32)
    inverse = jnp.exp(-(2.0 * freq_index / head_width) * jnp.log(jnp.float32(rope_base)))
    angles = token_positions.astype(jnp.float32)[:, None] * inverse[None, :]
    cosine = jnp.cos(angles)[:, None, :]
    sine_table = jnp.sin(angles)[:, None, :]
    shaped = values.reshape(values.shape[0], head_count, head_width)
    front_half = shaped[..., :half_width]
    back_half = shaped[..., half_width:]
    turned = jnp.concatenate([front_half * cosine - back_half * sine_table, back_half * cosine + front_half * sine_table], axis=-1)
    return turned.reshape(values.shape[0], head_count * head_width)


def attend_block(query_block_rows, key_span_rows, value_span_rows, allowed):
    total_row_count = query_block_rows.shape[0]
    window_key_count = key_span_rows.shape[0]
    query_group_width = QUERY_HEADS // KEY_VALUE_HEADS
    query_heads_view = query_block_rows.astype(jnp.float32).reshape(total_row_count, KEY_VALUE_HEADS, query_group_width, HEAD_SIZE)
    key_heads_view = key_span_rows.astype(jnp.float32).reshape(window_key_count, KEY_VALUE_HEADS, HEAD_SIZE)
    value_heads_view = value_span_rows.astype(jnp.float32).reshape(window_key_count, KEY_VALUE_HEADS, HEAD_SIZE)
    scores = jnp.einsum("rhgd,khd->hgrk", query_heads_view, key_heads_view) * (HEAD_SIZE ** -0.5)
    scores = jnp.where(allowed[None, None], scores, masked_score)
    largest = jnp.max(scores, axis=-1, keepdims=True)
    expo_terms = jnp.exp(scores - largest)
    denominator = jnp.sum(expo_terms, axis=-1, keepdims=True)
    weights = (expo_terms / denominator).astype(jnp.bfloat16)
    mixed = jnp.einsum("hgrk,khd->rhgd", weights.astype(jnp.float32), value_heads_view)
    return mixed.reshape(total_row_count, QUERY_HEADS * HEAD_SIZE).astype(jnp.bfloat16)


def reference(hidden, dest, doc_ids, w_query, key_weight, value_weight):
    ordered = jnp.zeros_like(hidden).at[dest].set(hidden)
    query_raw = jnp.dot(ordered, w_query, preferred_element_type=jnp.float32).astype(jnp.bfloat16)
    key_unrotated = jnp.dot(ordered, key_weight, preferred_element_type=jnp.float32).astype(jnp.bfloat16)
    value_matrix = jnp.dot(ordered, value_weight, preferred_element_type=jnp.float32).astype(jnp.bfloat16)
    token_positions = jnp.arange(SEQ, dtype=jnp.int32)
    queries = apply_rotation(query_raw.astype(jnp.float32), token_positions, QUERY_HEADS).astype(jnp.bfloat16)
    key_matrix = apply_rotation(key_unrotated.astype(jnp.float32), token_positions, KEY_VALUE_HEADS).astype(jnp.bfloat16)
    padded_keys = jnp.concatenate([jnp.zeros((BLOCK_TOKENS, KEY_VALUE_HEADS * HEAD_SIZE), jnp.bfloat16), key_matrix], axis=0)
    padded_values = jnp.concatenate([jnp.zeros((BLOCK_TOKENS, KEY_VALUE_HEADS * HEAD_SIZE), jnp.bfloat16), value_matrix], axis=0)
    pad_docs = jnp.concatenate([jnp.full((BLOCK_TOKENS,), -1, jnp.int32), doc_ids.astype(jnp.int32)], axis=0)
    local_index = jnp.arange(BLOCK_TOKENS, dtype=jnp.int32)
    across = jnp.arange(2 * BLOCK_TOKENS, dtype=jnp.int32)
    reach = (across[None, :] > local_index[:, None]) & (across[None, :] <= local_index[:, None] + BLOCK_TOKENS)

    def one_block(block):
        start = (block * BLOCK_TOKENS).astype(jnp.int32)
        query_block_rows = lax.dynamic_slice_in_dim(queries, start, BLOCK_TOKENS, 0)
        key_span_rows = lax.dynamic_slice_in_dim(padded_keys, start, 2 * BLOCK_TOKENS, 0)
        value_span_rows = lax.dynamic_slice_in_dim(padded_values, start, 2 * BLOCK_TOKENS, 0)
        query_docs = lax.dynamic_slice_in_dim(pad_docs, start + BLOCK_TOKENS, BLOCK_TOKENS, 0)
        key_docs = lax.dynamic_slice_in_dim(pad_docs, start, 2 * BLOCK_TOKENS, 0)
        allowed = reach & (query_docs[:, None] == key_docs[None, :])
        return attend_block(query_block_rows, key_span_rows, value_span_rows, allowed)

    blocks = lax.map(one_block, jnp.arange(N_CTX, dtype=jnp.int32))
    return blocks.reshape(SEQ, QUERY_HEADS * HEAD_SIZE)
```

```python
import functools

import jax
import jax.numpy as jnp
from jax import lax
from jax.experimental import pallas as pl
from jax.experimental.pallas import tpu as pltpu
from jax.sharding import PartitionSpec as P

HEAD = 128
ROPE_BASE = 500000.0 * 16.0 ** (128.0 / 126.0)
MASKED = -1e30
QT = 128
VMEM_LIMIT = 56 * 1024 * 1024


def params(n=1):
    return pltpu.CompilerParams(
        dimension_semantics=("arbitrary",) * n, vmem_limit_bytes=VMEM_LIMIT
    )


def project_kernel(koff, x0, x1, slots, *refs):
    *ws, out, y = refs
    i = pl.program_id(0)
    half = lax.rem(i, 2)
    bm = x0.shape[0]
    kk = ws[0].shape[0] // 2
    n = ws[0].shape[1]

    def compute(x):
        acc = jnp.zeros((bm, n), jnp.float32)
        for k, w in enumerate(ws):
            for h in range(2):
                off = pl.multiple_of(koff[2 * k + h], kk)
                acc = acc + jnp.dot(
                    x[:, pl.ds(off, kk)],
                    w[h * kk : (h + 1) * kk, :],
                    preferred_element_type=jnp.float32,
                )
        y[pl.ds(pl.multiple_of(half * bm, bm), bm), :] = acc.astype(y.dtype)

    @pl.when(i < 2)
    def _():
        compute(x0)

    @pl.when(i >= 2)
    def _():
        compute(x1)

    @pl.when(half == 1)
    def _():
        chips, _, per, _ = out.shape
        rows = y.shape[0]
        row_slot = slots[0]
        step = max(1, 256 // per)
        for a in range(0, chips, step):
            ids = lax.broadcasted_iota(jnp.int32, (step * per, rows), 0) + a * per
            pick = jnp.where(ids == row_slot, 1.0, 0.0).astype(y.dtype)
            part = jnp.dot(pick, y[...], preferred_element_type=jnp.float32)
            out[a : a + step, 0] = part.astype(out.dtype).reshape(step, per, n)


def project(x0, x1, slots, ws, koff, per):
    rows, width = x0.shape
    n = ws[0].shape[1]
    chips = len(ws)
    bm = rows // 2
    grid_spec = pltpu.PrefetchScalarGridSpec(
        num_scalar_prefetch=1,
        grid=(4,),
        in_specs=[
            pl.BlockSpec((bm, width), lambda i, s: (jnp.minimum(i, 1), 0)),
            pl.BlockSpec((bm, width), lambda i, s: (jnp.maximum(i - 2, 0), 0)),
            pl.BlockSpec((1, 1, rows), lambda i, s: (i // 2, 0, 0)),
        ]
        + [pl.BlockSpec(w.shape, lambda i, s: (0, 0)) for w in ws],
        out_specs=pl.BlockSpec((chips, 1, per, n), lambda i, s: (0, i // 2, 0, 0)),
        scratch_shapes=[pltpu.VMEM((rows, n), x0.dtype)],
    )
    return pl.pallas_call(
        project_kernel,
        grid_spec=grid_spec,
        out_shape=jax.ShapeDtypeStruct((chips, 2, per, n), x0.dtype),
        compiler_params=params(),
        name="project",
    )(koff, x0, x1, slots, *ws)


def unpack_rows(got, target, rows):
    slots = got.shape[0]
    ids = lax.broadcasted_iota(jnp.int32, (rows, slots), 0)
    pick = jnp.where(ids == target, 1.0, 0.0).astype(got.dtype)
    return jnp.dot(pick, got, preferred_element_type=jnp.float32)


def rotated(v, cosine, sine):
    return v * cosine + pltpu.roll(v, HEAD // 2, 1) * sine


def keys_kernel(core, got, target, cosine, sine, out):
    rows = out.shape[1]
    v = unpack_rows(got[...].reshape(-1, got.shape[-1]), target[0], rows)
    out[0, :, :HEAD] = rotated(v[:, :HEAD], cosine[...], sine[...]).astype(out.dtype)
    out[0, :, HEAD:] = v[:, HEAD:].astype(out.dtype)


def unpack_keys(core, got, target, cosine, sine, rows):
    chips, _, _, cap, n = got.shape
    grid_spec = pltpu.PrefetchScalarGridSpec(
        num_scalar_prefetch=1,
        grid=(2,),
        in_specs=[
            pl.BlockSpec((chips, 2, 1, cap, n), lambda e, s: (0, 0, e ^ s[0], 0, 0)),
            pl.BlockSpec((1, 1, chips * 2 * cap), lambda e, s: (e ^ s[0], 0, 0)),
            pl.BlockSpec((rows, HEAD), lambda e, s: (e, 0)),
            pl.BlockSpec((rows, HEAD), lambda e, s: (e, 0)),
        ],
        out_specs=pl.BlockSpec((1, rows, n), lambda e, s: (e, 0, 0)),
    )
    return pl.pallas_call(
        keys_kernel,
        grid_spec=grid_spec,
        out_shape=jax.ShapeDtypeStruct((2, rows, n), got.dtype),
        compiler_params=params(),
        name="keys",
    )(core, got, target, cosine, sine)


def attend_kernel(core, got, target, prior, own, cosine, sine, qdocs, kdocs, out, q, kv):
    rows = out.shape[0]
    heads = got.shape[-1] // HEAD
    span = rows + QT
    v = unpack_rows(got[...].reshape(-1, got.shape[-1]), target[0], rows)
    for h in range(heads):
        q[h] = rotated(v[:, h * HEAD : (h + 1) * HEAD], cosine[...], sine[...]).astype(q.dtype)
    kv[:rows] = prior[0]
    kv[rows:] = own[0]
    scale = HEAD**-0.5

    def tile(i, carry):
        at = pl.multiple_of(i * QT, QT)
        qs = q[:, pl.ds(at, QT), :].reshape(heads * QT, HEAD)
        ks = kv[pl.ds(at, span), :HEAD]
        vs = kv[pl.ds(at, span), HEAD:]
        s = lax.dot_general(
            qs, ks, (((1,), (1,)), ((), ())), preferred_element_type=jnp.float32
        ).reshape(heads, QT, span)
        behind = lax.broadcasted_iota(jnp.int32, (QT, span), 1) - lax.broadcasted_iota(
            jnp.int32, (QT, span), 0
        )
        ok = (behind > 0) & (behind <= rows) & (
            qdocs[pl.ds(at, QT), :1] == kdocs[0, :, pl.ds(at, span)]
        )
        s = jnp.where(ok[None], s * scale, MASKED)
        top = jnp.max(s, axis=-1, keepdims=True)
        w = jnp.exp(s - top)
        total = jnp.sum(w, axis=-1, keepdims=True)
        o = jnp.dot(
            w.astype(kv.dtype).reshape(heads * QT, span), vs, preferred_element_type=jnp.float32
        ).reshape(heads, QT, HEAD)
        o = o / total
        for h in range(heads):
            out[pl.ds(at, QT), h * HEAD : (h + 1) * HEAD] = o[h].astype(out.dtype)
        return carry

    lax.fori_loop(0, rows // QT, tile, 0)


def attend(d, core, got, target, kv3, cosine, sine, qdocs, kdocs, rows):
    chips, _, _, cap, n = got.shape
    grid_spec = pltpu.PrefetchScalarGridSpec(
        num_scalar_prefetch=1,
        grid=(1,),
        in_specs=[
            pl.BlockSpec((chips, 2, 1, cap, n), lambda i, s: (0, 0, d, 0, 0)),
            pl.BlockSpec((1, 1, chips * 2 * cap), lambda i, s: (d, 0, 0)),
            pl.BlockSpec((1, rows, 2 * HEAD), lambda i, s: (d ^ s[0], 0, 0)),
            pl.BlockSpec((1, rows, 2 * HEAD), lambda i, s: ((d ^ s[0]) + 1, 0, 0)),
            pl.BlockSpec((rows, HEAD), lambda i, s: (d ^ s[0], 0)),
            pl.BlockSpec((rows, HEAD), lambda i, s: (d ^ s[0], 0)),
            pl.BlockSpec((rows, HEAD), lambda i, s: (d ^ s[0], 0)),
            pl.BlockSpec((1, 1, 2 * rows), lambda i, s: (d ^ s[0], 0, 0)),
        ],
        out_specs=pl.BlockSpec((rows, n), lambda i, s: (0, 0)),
        scratch_shapes=[
            pltpu.VMEM((n // HEAD, rows, HEAD), got.dtype),
            pltpu.VMEM((2 * rows, 2 * HEAD), got.dtype),
        ],
    )
    return pl.pallas_call(
        attend_kernel,
        grid_spec=grid_spec,
        out_shape=jax.ShapeDtypeStruct((rows, n), got.dtype),
        compiler_params=params(),
        name="attend",
    )(core, got, target, kv3, kv3, cosine, sine, qdocs, kdocs)


def join_kernel(place, a, b, c, d, out):
    i = pl.program_id(0)
    for k, piece in enumerate((a, b, c, d)):

        @pl.when(i == k)
        def _(piece=piece):
            out[...] = piece[...]


def join(part, pieces):
    rows, n = pieces[0].shape
    grid_spec = pltpu.PrefetchScalarGridSpec(
        num_scalar_prefetch=1,
        grid=(len(pieces),),
        in_specs=[pl.BlockSpec((rows, n), lambda i, s: (0, 0)) for _ in pieces],
        out_specs=pl.BlockSpec((rows, n), lambda i, s: (0, s[0] ^ i)),
    )
    return pl.pallas_call(
        join_kernel,
        grid_spec=grid_spec,
        out_shape=jax.ShapeDtypeStruct((rows, n * len(pieces)), pieces[0].dtype),
        compiler_params=params(),
        name="join",
    )(part, *pieces)


def chip_cycle(chips):
    return list(range(0, chips, 2)) + list(range(chips - 1 - chips % 2, 0, -2))


def ring_gather(shard, chips):
    order = chip_cycle(chips)

    def pairs(step):
        return [
            (2 * order[i] + c, 2 * order[(i + step) % chips] + c)
            for i in range(chips)
            for c in range(2)
        ]

    forth, back = pairs(1), pairs(-1)
    found = [shard]
    a = b = shard
    for hop in range(chips // 2):
        a = lax.ppermute(a, "ctx", forth)
        found.append(a)
        if hop < (chips - 1) // 2:
            b = lax.ppermute(b, "ctx", back)
            found.append(b)
    return found


def ring_sources(chip, chips):
    order = jnp.array(chip_cycle(chips), jnp.int32)
    place = jnp.sum(jnp.where(order == chip, jnp.arange(chips, dtype=jnp.int32), 0))
    steps = [0]
    for hop in range(chips // 2):
        steps.append(-(hop + 1))
        if hop < (chips - 1) // 2:
            steps.append(hop + 1)
    return order[(place + jnp.array(steps, jnp.int32)) % chips]


def on_device(hidden, dest, doc_ids, w_query, key_weight, value_weight):
    rows = hidden.shape[0]
    dp = lax.axis_size("dp")
    size = lax.axis_size("ctx")
    chips = size // 2
    cap = 2 * rows // size
    index = lax.axis_index("ctx")
    chip = index // 2
    core = index % 2
    part = (lax.axis_index("dp") % 2) * 2 + core
    parts = 4
    kq = w_query.shape[1] // parts
    kk = key_weight.shape[1] // parts
    depth = w_query.shape[0]

    core_pairs = [(i, i ^ 1) for i in range(size)]
    side_pairs = [(i, i ^ 1) for i in range(dp)]
    same_core = [[2 * i + c for i in range(chips)] for c in range(2)]

    def to_core(x):
        return lax.ppermute(x, "ctx", core_pairs)

    def to_side(x):
        return lax.ppermute(x, "dp", side_pairs)

    def exchange(x):
        return lax.all_to_all(
            x, "ctx", split_axis=0, concat_axis=0, tiled=True, axis_index_groups=same_core
        )

    def columns(g):
        return jnp.concatenate(
            [
                lax.dynamic_slice_in_dim(key_weight, g * kk, kk, 1),
                lax.dynamic_slice_in_dim(value_weight, g * kk, kk, 1),
                lax.dynamic_slice_in_dim(w_query, g * kq, kq, 1),
            ],
            axis=1,
        )

    shard = jnp.concatenate([columns(part), to_core(columns(part ^ 1))], axis=0)
    ws_kv = ring_gather(shard[:, : 2 * kk], chips)
    ws_q = ring_gather(shard[:, 2 * kk :], chips)
    sources = ring_sources(chip, chips)
    koff = (
        jnp.stack([2 * sources + core, 2 * sources + 1 - core], axis=1).reshape(-1) * depth
    ).astype(jnp.int32)

    beside = to_side(hidden)
    xs = ((hidden, to_core(hidden)), (beside, to_core(beside)))

    table = lax.all_to_all(
        jnp.broadcast_to(dest[None], (size, rows)), "ctx", split_axis=0, concat_axis=0, tiled=True
    )
    tables = jnp.stack([table, to_side(table)]).reshape(2, chips, 2, rows)
    tables = jnp.where(core == 0, tables, tables[:, :, ::-1])
    block = tables // rows
    local = tables % rows
    before = (
        jnp.arange(rows, dtype=jnp.int32)[:, None] < jnp.arange(rows, dtype=jnp.int32)[None, :]
    ).astype(jnp.bfloat16)

    def rank_in(hit):
        return jnp.dot(
            hit.astype(jnp.bfloat16), before, preferred_element_type=jnp.float32
        ).astype(jnp.int32)

    leaving = lax.dynamic_index_in_dim(block, chip, 1, keepdims=False)
    hit = leaving[:, :, None, :] == jnp.arange(size, dtype=jnp.int32)[None, None, :, None]
    rank = jnp.sum(jnp.where(hit, rank_in(hit), 0), axis=2)
    slots = (leaving // 2) * (2 * cap) + ((leaving % 2) ^ core) * cap + rank
    slots = slots.reshape(2, 2, 1, rows)

    mine = 2 * chip + (jnp.arange(2, dtype=jnp.int32) ^ core)
    hit = block[:, None] == mine[None, :, None, None, None]
    rank = rank_in(hit)
    at_slot = hit[..., None, :] & (
        rank[..., None, :] == jnp.arange(cap, dtype=jnp.int32)[:, None]
    )
    targets = jnp.sum(jnp.where(at_slot, local[:, None, :, :, None, :] + 1, 0), axis=-1) - 1
    targets = targets.reshape(2, 2, 1, size * cap)

    half = HEAD // 2
    freq = jnp.arange(half, dtype=jnp.float32)
    inverse = jnp.exp(-(2.0 * freq / HEAD) * jnp.log(jnp.float32(ROPE_BASE)))
    positions = chip * 2 * rows + jnp.arange(2 * rows, dtype=jnp.int32)
    angles = positions.astype(jnp.float32)[:, None] * inverse[None, :]
    cos_half, sin_half = jnp.cos(angles), jnp.sin(angles)
    cosine = jnp.concatenate([cos_half, cos_half], axis=1)
    sine = jnp.concatenate([-sin_half, sin_half], axis=1)
    core_ref = core.reshape(1).astype(jnp.int32)

    def doc_tables(docs):
        padded = jnp.concatenate([jnp.full((rows,), -1, jnp.int32), docs])
        near = lax.dynamic_slice_in_dim(padded, chip * 2 * rows, 3 * rows, 0)
        qdocs = jnp.broadcast_to(near[rows:, None], (2 * rows, HEAD))
        kdocs = jnp.stack([near[: 2 * rows], near[rows:]])[:, None, :]
        return qdocs, kdocs

    docs = (doc_tables(doc_ids), doc_tables(to_side(doc_ids)))
    ahead = [(i, i + 2) for i in range(size - 2)]

    def send(t, ws):
        out = project(*xs[t], slots[t], ws, koff, 2 * cap)
        got = exchange(out.reshape(chips, 4 * cap, out.shape[-1]))
        return got.reshape(chips, 2, 2, cap, out.shape[-1])

    def keys_of(t, got):
        kv = unpack_keys(core_ref, got, targets[t], cosine, sine, rows)
        return jnp.concatenate([lax.ppermute(kv[1:], "ctx", ahead), kv], axis=0)

    def result(t, d, got, kv3):
        return attend(d, core_ref, got, targets[t], kv3, cosine, sine, *docs[t], rows)

    kv_own = keys_of(0, send(0, ws_kv))
    kv_side = keys_of(1, send(1, ws_kv))
    got_side = send(1, ws_q)
    got_own = send(0, ws_q)
    far = to_core(to_side(result(1, 1, got_side, kv_side)))
    near = to_side(result(1, 0, got_side, kv_side))
    other = to_core(result(0, 1, got_own, kv_own))
    own = result(0, 0, got_own, kv_own)
    return join(part.reshape(1).astype(jnp.int32), (own, other, near, far))


def solution(mesh):
    placed = (
        P(("dp", "ctx"), None),
        P(("dp", "ctx")),
        P("dp"),
        P("ctx", None),
        P("ctx", None),
        P("ctx", None),
    )
    return jax.shard_map(
        on_device, mesh=mesh, in_specs=placed, out_specs=P(("dp", "ctx"), None), check_vma=False
    )
```

```python
import functools

import jax
import jax.numpy as jnp
from jax import lax
from jax.experimental import pallas as pl
from jax.experimental.pallas import tpu as pltpu
from jax.sharding import PartitionSpec as P


HEAD = 128
ROPE_BASE = 500000.0 * 16.0 ** (128.0 / 126.0)
MASKED = -1e30
QT = 128
VMEM_LIMIT = 56 * 1024 * 1024


def params(n=1):
    return pltpu.CompilerParams(
        dimension_semantics=("arbitrary",) * n, vmem_limit_bytes=VMEM_LIMIT
    )


def project_kernel(koff, x0, x1, slots, *refs):
    *ws, out, y = refs
    i = pl.program_id(0)
    half = lax.rem(i, 2)
    bm = x0.shape[0]
    kk = ws[0].shape[0] // 2
    n = ws[0].shape[1]

    def compute(x):
        acc = jnp.zeros((bm, n), jnp.float32)
        for k, w in enumerate(ws):
            for h in range(2):
                off = pl.multiple_of(koff[2 * k + h], kk)
                acc = acc + jnp.dot(
                    x[:, pl.ds(off, kk)],
                    w[h * kk : (h + 1) * kk, :],
                    preferred_element_type=jnp.float32,
                )
        y[pl.ds(pl.multiple_of(half * bm, bm), bm), :] = acc.astype(y.dtype)

    @pl.when(i < 2)
    def _():
        compute(x0)

    @pl.when(i >= 2)
    def _():
        compute(x1)

    @pl.when(half == 1)
    def _():
        chips, _, per, _ = out.shape
        rows = y.shape[0]
        row_slot = slots[0]
        step = max(1, 256 // per)
        for a in range(0, chips, step):
            ids = lax.broadcasted_iota(jnp.int32, (step * per, rows), 0) + a * per
            pick = jnp.where(ids == row_slot, 1.0, 0.0).astype(y.dtype)
            part = jnp.dot(pick, y[...], preferred_element_type=jnp.float32)
            out[a : a + step, 0] = part.astype(out.dtype).reshape(step, per, n)


def project(x0, x1, slots, ws, koff, per):
    rows, width = x0.shape
    n = ws[0].shape[1]
    chips = len(ws)
    bm = rows // 2
    grid_spec = pltpu.PrefetchScalarGridSpec(
        num_scalar_prefetch=1,
        grid=(4,),
        in_specs=[
            pl.BlockSpec((bm, width), lambda i, s: (jnp.minimum(i, 1), 0)),
            pl.BlockSpec((bm, width), lambda i, s: (jnp.maximum(i - 2, 0), 0)),
            pl.BlockSpec((1, 1, rows), lambda i, s: (i // 2, 0, 0)),
        ]
        + [pl.BlockSpec(w.shape, lambda i, s: (0, 0)) for w in ws],
        out_specs=pl.BlockSpec((chips, 1, per, n), lambda i, s: (0, i // 2, 0, 0)),
        scratch_shapes=[pltpu.VMEM((rows, n), x0.dtype)],
    )
    return pl.pallas_call(
        project_kernel,
        grid_spec=grid_spec,
        out_shape=jax.ShapeDtypeStruct((chips, 2, per, n), x0.dtype),
        compiler_params=params(),
        name="project",
    )(koff, x0, x1, slots, *ws)


def unpack_rows(got, target, rows):
    slots = got.shape[0]
    ids = lax.broadcasted_iota(jnp.int32, (rows, slots), 0)
    pick = jnp.where(ids == target, 1.0, 0.0).astype(got.dtype)
    return jnp.dot(pick, got, preferred_element_type=jnp.float32)


def rotated(v, cosine, sine):
    return v * cosine + pltpu.roll(v, HEAD // 2, 1) * sine


def keys_kernel(core, got, target, cosine, sine, first, second):
    v = unpack_rows(got[...].reshape(-1, got.shape[-1]), target[0], first.shape[0])
    k = rotated(v[:, :HEAD], cosine[...], sine[...])
    for e, out in enumerate((first, second)):

        @pl.when(pl.program_id(0) == e)
        def _(out=out):
            out[:, :HEAD] = k.astype(out.dtype)
            out[:, HEAD:] = v[:, HEAD:].astype(out.dtype)


def unpack_keys(core, got, target, cosine, sine, rows):
    chips, _, _, cap, n = got.shape
    grid_spec = pltpu.PrefetchScalarGridSpec(
        num_scalar_prefetch=1,
        grid=(2,),
        in_specs=[
            pl.BlockSpec((chips, 2, 1, cap, n), lambda e, s: (0, 0, e ^ s[0], 0, 0)),
            pl.BlockSpec((1, 1, chips * 2 * cap), lambda e, s: (e ^ s[0], 0, 0)),
            pl.BlockSpec((rows, HEAD), lambda e, s: (e, 0)),
            pl.BlockSpec((rows, HEAD), lambda e, s: (e, 0)),
        ],
        out_specs=[pl.BlockSpec((rows, n), lambda e, s: (0, 0))] * 2,
    )
    return pl.pallas_call(
        keys_kernel,
        grid_spec=grid_spec,
        out_shape=[jax.ShapeDtypeStruct((rows, n), got.dtype)] * 2,
        compiler_params=params(),
        name="keys",
    )(core, got, target, cosine, sine)


def attend_kernel(d, core, got, target, *refs):
    *blocks, cosine, sine, qdocs, kdocs, out, q, kv = refs
    rows = out.shape[0]
    heads = got.shape[-1] // HEAD
    span = rows + QT
    v = unpack_rows(got[...].reshape(-1, got.shape[-1]), target[0], rows)
    for h in range(heads):
        q[h] = rotated(v[:, h * HEAD : (h + 1) * HEAD], cosine[...], sine[...]).astype(q.dtype)
    for e in range(2):

        @pl.when(d ^ core[0] == e)
        def _(e=e):
            kv[:rows] = blocks[e][...]
            kv[rows:] = blocks[e + 1][...]

    scale = HEAD**-0.5

    def tile(i, carry):
        at = pl.multiple_of(i * QT, QT)
        qs = q[:, pl.ds(at, QT), :].reshape(heads * QT, HEAD)
        ks = kv[pl.ds(at, span), :HEAD]
        vs = kv[pl.ds(at, span), HEAD:]
        s = lax.dot_general(
            qs, ks, (((1,), (1,)), ((), ())), preferred_element_type=jnp.float32
        ).reshape(heads, QT, span)
        behind = lax.broadcasted_iota(jnp.int32, (QT, span), 1) - lax.broadcasted_iota(
            jnp.int32, (QT, span), 0
        )
        ok = (behind > 0) & (behind <= rows) & (
            qdocs[pl.ds(at, QT), :1] == kdocs[0, :, pl.ds(at, span)]
        )
        s = jnp.where(ok[None], s * scale, MASKED)
        top = jnp.max(s, axis=-1, keepdims=True)
        w = jnp.exp(s - top)
        total = jnp.sum(w, axis=-1, keepdims=True)
        o = jnp.dot(
            w.astype(kv.dtype).reshape(heads * QT, span), vs, preferred_element_type=jnp.float32
        ).reshape(heads, QT, HEAD)
        o = o / total
        for h in range(heads):
            out[pl.ds(at, QT), h * HEAD : (h + 1) * HEAD] = o[h].astype(out.dtype)
        return carry

    lax.fori_loop(0, rows // QT, tile, 0)


def attend(d, core, got, target, kv3, cosine, sine, qdocs, kdocs, rows):
    chips, _, _, cap, n = got.shape
    grid_spec = pltpu.PrefetchScalarGridSpec(
        num_scalar_prefetch=1,
        grid=(1,),
        in_specs=[
            pl.BlockSpec((chips, 2, 1, cap, n), lambda i, s: (0, 0, d, 0, 0)),
            pl.BlockSpec((1, 1, chips * 2 * cap), lambda i, s: (d, 0, 0)),
            *[pl.BlockSpec((rows, 2 * HEAD), lambda i, s: (0, 0))] * 3,
            pl.BlockSpec((rows, HEAD), lambda i, s: (d ^ s[0], 0)),
            pl.BlockSpec((rows, HEAD), lambda i, s: (d ^ s[0], 0)),
            pl.BlockSpec((rows, HEAD), lambda i, s: (d ^ s[0], 0)),
            pl.BlockSpec((1, 1, 2 * rows), lambda i, s: (d ^ s[0], 0, 0)),
        ],
        out_specs=pl.BlockSpec((rows, n), lambda i, s: (0, 0)),
        scratch_shapes=[
            pltpu.VMEM((n // HEAD, rows, HEAD), got.dtype),
            pltpu.VMEM((2 * rows, 2 * HEAD), got.dtype),
        ],
    )
    return pl.pallas_call(
        functools.partial(attend_kernel, d),
        grid_spec=grid_spec,
        out_shape=jax.ShapeDtypeStruct((rows, n), got.dtype),
        compiler_params=params(),
        name="attend",
    )(core, got, target, *kv3, cosine, sine, qdocs, kdocs)


def join_kernel(place, a, b, c, d, out):
    i = pl.program_id(0)
    for k, piece in enumerate((a, b, c, d)):

        @pl.when(i == k)
        def _(piece=piece):
            out[...] = piece[...]


def join(part, pieces):
    rows, n = pieces[0].shape
    grid_spec = pltpu.PrefetchScalarGridSpec(
        num_scalar_prefetch=1,
        grid=(len(pieces),),
        in_specs=[pl.BlockSpec((rows, n), lambda i, s: (0, 0)) for _ in pieces],
        out_specs=pl.BlockSpec((rows, n), lambda i, s: (0, s[0] ^ i)),
    )
    return pl.pallas_call(
        join_kernel,
        grid_spec=grid_spec,
        out_shape=jax.ShapeDtypeStruct((rows, n * len(pieces)), pieces[0].dtype),
        compiler_params=params(),
        name="join",
    )(part, *pieces)


def chip_cycle(chips):
    return list(range(0, chips, 2)) + list(range(chips - 1 - chips % 2, 0, -2))


def ring_gather(shard, chips):
    order = chip_cycle(chips)

    def pairs(step):
        return [
            (2 * order[i] + c, 2 * order[(i + step) % chips] + c)
            for i in range(chips)
            for c in range(2)
        ]

    forth, back = pairs(1), pairs(-1)
    found = [shard]
    a = b = shard
    for hop in range(chips // 2):
        a = lax.ppermute(a, "ctx", forth)
        found.append(a)
        if hop < (chips - 1) // 2:
            b = lax.ppermute(b, "ctx", back)
            found.append(b)
    return found


def ring_sources(chip, chips):
    order = jnp.array(chip_cycle(chips), jnp.int32)
    place = jnp.sum(jnp.where(order == chip, jnp.arange(chips, dtype=jnp.int32), 0))
    steps = [0]
    for hop in range(chips // 2):
        steps.append(-(hop + 1))
        if hop < (chips - 1) // 2:
            steps.append(hop + 1)
    return order[(place + jnp.array(steps, jnp.int32)) % chips]


def layer(hidden, dest, doc_ids, w_query, key_weight, value_weight):
    rows = hidden.shape[0]
    dp = lax.axis_size("dp")
    size = lax.axis_size("ctx")
    chips = size // 2
    cap = 2 * rows // size
    index = lax.axis_index("ctx")
    chip = index // 2
    core = index % 2
    part = (lax.axis_index("dp") % 2) * 2 + core
    parts = 4
    kq = w_query.shape[1] // parts
    kk = key_weight.shape[1] // parts
    depth = w_query.shape[0]

    core_pairs = [(i, i ^ 1) for i in range(size)]
    side_pairs = [(i, i ^ 1) for i in range(dp)]
    same_core = [[2 * i + c for i in range(chips)] for c in range(2)]

    def to_core(x):
        return lax.ppermute(x, "ctx", core_pairs)

    def to_side(x):
        return lax.ppermute(x, "dp", side_pairs)

    def exchange(x):
        return lax.all_to_all(
            x, "ctx", split_axis=0, concat_axis=0, tiled=True, axis_index_groups=same_core
        )

    ints = to_side(jnp.concatenate([dest, doc_ids]))
    beside = to_side(hidden)

    def columns(g):
        return jnp.concatenate(
            [
                lax.dynamic_slice_in_dim(key_weight, g * kk, kk, 1),
                lax.dynamic_slice_in_dim(value_weight, g * kk, kk, 1),
                lax.dynamic_slice_in_dim(w_query, g * kq, kq, 1),
            ],
            axis=1,
        )

    shard = jnp.concatenate([columns(part), to_core(columns(part ^ 1))], axis=0)
    ws_kv = ring_gather(shard[:, : 2 * kk], chips)
    ws_q = ring_gather(shard[:, 2 * kk :], chips)
    sources = ring_sources(chip, chips)
    koff = (
        jnp.stack([2 * sources + core, 2 * sources + 1 - core], axis=1).reshape(-1) * depth
    ).astype(jnp.int32)

    across = to_core(hidden)
    diagonal = to_core(beside)
    xs = ((hidden, across), (beside, diagonal))

    both = jnp.stack([dest, ints[:rows]])
    tables = lax.all_to_all(
        jnp.broadcast_to(both[None], (size, 2, rows)),
        "ctx",
        split_axis=0,
        concat_axis=0,
        tiled=True,
    )
    tables = jnp.moveaxis(tables, 1, 0).reshape(2, chips, 2, rows)
    tables = jnp.where(core == 0, tables, tables[:, :, ::-1])
    block = tables // rows
    local = tables % rows
    before = (
        jnp.arange(rows, dtype=jnp.int32)[:, None] < jnp.arange(rows, dtype=jnp.int32)[None, :]
    ).astype(jnp.bfloat16)

    def rank_in(hit):
        return jnp.dot(
            hit.astype(jnp.bfloat16), before, preferred_element_type=jnp.float32
        ).astype(jnp.int32)

    leaving = lax.dynamic_index_in_dim(block, chip, 1, keepdims=False)
    hit = leaving[:, :, None, :] == jnp.arange(size, dtype=jnp.int32)[None, None, :, None]
    rank = jnp.sum(jnp.where(hit, rank_in(hit), 0), axis=2)
    slots = (leaving // 2) * (2 * cap) + ((leaving % 2) ^ core) * cap + rank
    slots = slots.reshape(2, 2, 1, rows)

    mine = 2 * chip + (jnp.arange(2, dtype=jnp.int32) ^ core)
    hit = block[:, None] == mine[None, :, None, None, None]
    rank = rank_in(hit)
    at_slot = hit[..., None, :] & (
        rank[..., None, :] == jnp.arange(cap, dtype=jnp.int32)[:, None]
    )
    targets = jnp.sum(jnp.where(at_slot, local[:, None, :, :, None, :] + 1, 0), axis=-1) - 1
    targets = targets.reshape(2, 2, 1, size * cap)

    half = HEAD // 2
    freq = jnp.arange(half, dtype=jnp.float32)
    inverse = jnp.exp(-(2.0 * freq / HEAD) * jnp.log(jnp.float32(ROPE_BASE)))
    positions = chip * 2 * rows + jnp.arange(2 * rows, dtype=jnp.int32)
    angles = positions.astype(jnp.float32)[:, None] * inverse[None, :]
    cos_half, sin_half = jnp.cos(angles), jnp.sin(angles)
    cosine = jnp.concatenate([cos_half, cos_half], axis=1)
    sine = jnp.concatenate([-sin_half, sin_half], axis=1)
    core_ref = core.reshape(1).astype(jnp.int32)

    def doc_tables(docs):
        padded = jnp.concatenate([jnp.full((rows,), -1, jnp.int32), docs])
        near = lax.dynamic_slice_in_dim(padded, chip * 2 * rows, 3 * rows, 0)
        qdocs = jnp.broadcast_to(near[rows:, None], (2 * rows, HEAD))
        kdocs = jnp.stack([near[: 2 * rows], near[rows:]])[:, None, :]
        return qdocs, kdocs

    docs = (doc_tables(doc_ids), doc_tables(ints[rows:]))
    ahead = [(i, i + 2) for i in range(size - 2)]

    def send(t, ws):
        out = project(*xs[t], slots[t], ws, koff, 2 * cap)
        got = exchange(out.reshape(chips, 4 * cap, out.shape[-1]))
        return got.reshape(chips, 2, 2, cap, out.shape[-1])

    def keys_of(t, got):
        first, second = unpack_keys(core_ref, got, targets[t], cosine, sine, rows)
        return lax.ppermute(second, "ctx", ahead), first, second

    def result(t, d, got, kv3):
        return attend(d, core_ref, got, targets[t], kv3, cosine, sine, *docs[t], rows)

    kv_own = keys_of(0, send(0, ws_kv))
    kv_side = keys_of(1, send(1, ws_kv))
    got_side = send(1, ws_q)
    got_own = send(0, ws_q)
    far = to_side(result(1, 1, got_side, kv_side))
    far = to_core(far)
    near = to_side(result(1, 0, got_side, kv_side))
    other = to_core(result(0, 1, got_own, kv_own))
    own = result(0, 0, got_own, kv_own)
    return join(part.reshape(1).astype(jnp.int32), (own, other, near, far))


def solution(mesh):
    placed = (
        P(("dp", "ctx"), None),
        P(("dp", "ctx")),
        P("dp"),
        P("ctx", None),
        P("ctx", None),
        P("ctx", None),
    )
    return jax.shard_map(
        layer, mesh=mesh, in_specs=placed, out_specs=P(("dp", "ctx"), None), check_vma=False
    )
```

```python
import functools

import jax
import jax.numpy as jnp
from jax import lax
from jax.experimental import pallas as pl
from jax.experimental.pallas import tpu as pltpu
from jax.sharding import PartitionSpec as P


HEAD = 128
ROPE_BASE = 500000.0 * 16.0 ** (128.0 / 126.0)
MASKED = -1e30
QT = 128
DP, CTX = "dp", "ctx"
VMEM_LIMIT = 56 * 1024 * 1024


def params(n=1):
    return pltpu.CompilerParams(
        dimension_semantics=("arbitrary",) * n, vmem_limit_bytes=VMEM_LIMIT
    )


def project_kernel(koff, x, slots, *refs):
    *refs, out, y = refs
    i = pl.program_id(0)
    chips, _, per, n = out.shape
    ws = refs[:chips]
    rows = y.shape[0]
    bm = x.shape[0]
    kk = ws[0].shape[0] // 2
    acc = jnp.zeros((bm, n), jnp.float32)
    for k, w in enumerate(ws):
        for h in range(2):
            off = pl.multiple_of(koff[2 * k + h], kk)
            acc = acc + jnp.dot(
                x[:, pl.ds(off, kk)],
                w[h * kk : (h + 1) * kk, :],
                preferred_element_type=jnp.float32,
            )
    y[pl.ds(pl.multiple_of(i * bm, bm), bm), :] = acc.astype(y.dtype)

    @pl.when(i == rows // bm - 1)
    def _():
        step = max(1, 256 // per)
        for a in range(0, chips, step):
            ids = lax.broadcasted_iota(jnp.int32, (step * per, rows), 0) + a * per
            pick = jnp.where(ids == slots[0], 1.0, 0.0).astype(y.dtype)
            part = jnp.dot(pick, y[...], preferred_element_type=jnp.float32)
            out[a : a + step, 0] = part.astype(out.dtype).reshape(step, per, n)


def project(x, slots, ws, koff, per, s, base=None):
    rows, width = x.shape
    n = ws[0].shape[1]
    chips = len(ws)
    bm = rows // 2
    more = [] if base is None else [base]
    grid_spec = pltpu.PrefetchScalarGridSpec(
        num_scalar_prefetch=1,
        grid=(2,),
        in_specs=[
            pl.BlockSpec((bm, width), lambda i, k: (i, 0)),
            pl.BlockSpec((1, 1, rows), lambda i, k: (s, 0, 0)),
        ]
        + [pl.BlockSpec(w.shape, lambda i, k: (0, 0)) for w in ws]
        + [pl.BlockSpec(memory_space=pl.ANY) for _ in more],
        out_specs=pl.BlockSpec((chips, 1, per, n), lambda i, k: (0, s, 0, 0)),
        scratch_shapes=[pltpu.VMEM((rows, n), x.dtype)],
    )
    return pl.pallas_call(
        project_kernel,
        grid_spec=grid_spec,
        out_shape=jax.ShapeDtypeStruct((chips, 2, per, n), x.dtype),
        input_output_aliases={3 + chips: 0} if more else {},
        compiler_params=params(),
    )(koff, x, slots, *ws, *more)


def unpack_rows(got, target, rows):
    slots = got.shape[0]
    ids = lax.broadcasted_iota(jnp.int32, (rows, slots), 0)
    pick = jnp.where(ids == target, 1.0, 0.0).astype(got.dtype)
    return jnp.dot(pick, got, preferred_element_type=jnp.float32)


def rotated(v, cosine, sine):
    return v * cosine + pltpu.roll(v, HEAD // 2, 1) * sine


def keys_kernel(core, got, target, cosine, sine, first, second):
    v = unpack_rows(got[...].reshape(-1, got.shape[-1]), target[0], first.shape[0])
    k = rotated(v[:, :HEAD], cosine[...], sine[...])
    for e, out in enumerate((first, second)):

        @pl.when(pl.program_id(0) == e)
        def _(out=out):
            out[:, :HEAD] = k.astype(out.dtype)
            out[:, HEAD:] = v[:, HEAD:].astype(out.dtype)


def unpack_keys(core, got, target, cosine, sine, rows):
    chips, _, _, cap, n = got.shape
    grid_spec = pltpu.PrefetchScalarGridSpec(
        num_scalar_prefetch=1,
        grid=(2,),
        in_specs=[
            pl.BlockSpec((chips, 2, 1, cap, n), lambda e, s: (0, 0, e ^ s[0], 0, 0)),
            pl.BlockSpec((1, 1, chips * 2 * cap), lambda e, s: (e ^ s[0], 0, 0)),
            pl.BlockSpec((rows, HEAD), lambda e, s: (e, 0)),
            pl.BlockSpec((rows, HEAD), lambda e, s: (e, 0)),
        ],
        out_specs=[pl.BlockSpec((rows, n), lambda e, s: (0, 0))] * 2,
    )
    return pl.pallas_call(
        keys_kernel,
        grid_spec=grid_spec,
        out_shape=[jax.ShapeDtypeStruct((rows, n), got.dtype)] * 2,
        compiler_params=params(),
    )(core, got, target, cosine, sine)


def attend_kernel(d, core, got, target, *refs):
    *refs, out, q, kv = refs
    *blocks, cosine, sine, qdocs, kdocs = refs[:7]
    rows = out.shape[0]
    heads = got.shape[-1] // HEAD
    span = rows + QT
    v = unpack_rows(got[...].reshape(-1, got.shape[-1]), target[0], rows)
    for h in range(heads):
        q[h] = rotated(v[:, h * HEAD : (h + 1) * HEAD], cosine[...], sine[...]).astype(q.dtype)
    for e in range(2):

        @pl.when(d ^ core[0] == e)
        def _(e=e):
            kv[:rows] = blocks[e][...]
            kv[rows:] = blocks[e + 1][...]

    scale = HEAD**-0.5

    def tile(i, carry):
        at = pl.multiple_of(i * QT, QT)
        qs = q[:, pl.ds(at, QT), :].reshape(heads * QT, HEAD)
        ks = kv[pl.ds(at, span), :HEAD]
        vs = kv[pl.ds(at, span), HEAD:]
        s = lax.dot_general(
            qs, ks, (((1,), (1,)), ((), ())), preferred_element_type=jnp.float32
        ).reshape(heads, QT, span)
        behind = lax.broadcasted_iota(jnp.int32, (QT, span), 1) - lax.broadcasted_iota(
            jnp.int32, (QT, span), 0
        )
        ok = (behind > 0) & (behind <= rows) & (
            qdocs[pl.ds(at, QT), :1] == kdocs[0, :, pl.ds(at, span)]
        )
        s = jnp.where(ok[None], s, MASKED)
        top = jnp.max(s, axis=-1, keepdims=True)
        w = jnp.exp((s - top) * scale)
        total = jnp.sum(w, axis=-1, keepdims=True)
        o = jnp.dot(
            w.astype(kv.dtype).reshape(heads * QT, span), vs, preferred_element_type=jnp.float32
        ).reshape(heads, QT, HEAD)
        o = o / total
        for h in range(heads):
            out[pl.ds(at, QT), h * HEAD : (h + 1) * HEAD] = o[h].astype(out.dtype)
        return carry

    lax.fori_loop(0, rows // QT, tile, 0, unroll=2)


def attend(d, scalars, got, target, kv3, cosine, sine, qdocs, kdocs, base=None):
    chips, _, _, cap, n = got.shape
    rows = kv3[0].shape[0]
    more = [] if base is None else [base]
    grid_spec = pltpu.PrefetchScalarGridSpec(
        num_scalar_prefetch=1,
        grid=(1,),
        in_specs=[
            pl.BlockSpec((chips, 2, 1, cap, n), lambda i, s: (0, 0, d, 0, 0)),
            pl.BlockSpec((1, 1, chips * 2 * cap), lambda i, s: (d, 0, 0)),
            *[pl.BlockSpec((rows, 2 * HEAD), lambda i, s: (0, 0))] * 3,
            *[pl.BlockSpec((rows, HEAD), lambda i, s: (d ^ s[0], 0))] * 3,
            pl.BlockSpec((1, 1, 2 * rows), lambda i, s: (d ^ s[0], 0, 0)),
            *[pl.BlockSpec(memory_space=pl.ANY) for _ in more],
        ],
        out_specs=pl.BlockSpec((rows, n), lambda i, s: (0, s[1] if more else 0)),
        scratch_shapes=[
            pltpu.VMEM((n // HEAD, rows, HEAD), got.dtype),
            pltpu.VMEM((2 * rows, 2 * HEAD), got.dtype),
        ],
    )
    shape = base.shape if more else (rows, n)
    return pl.pallas_call(
        functools.partial(attend_kernel, d),
        grid_spec=grid_spec,
        out_shape=jax.ShapeDtypeStruct(shape, got.dtype),
        input_output_aliases={10: 0} if more else {},
        compiler_params=params(),
    )(scalars, got, target, *kv3, cosine, sine, qdocs, kdocs, *more)


def place_kernel(count, scalars, *refs):
    out = refs[-1]
    for k in range(count):

        @pl.when(pl.program_id(0) == k)
        def _(piece=refs[k]):
            out[...] = piece[...]


def place(scalars, pieces, first, parts, base=None):
    rows, n = pieces[0].shape
    more = [] if base is None else [base]
    grid_spec = pltpu.PrefetchScalarGridSpec(
        num_scalar_prefetch=1,
        grid=(len(pieces),),
        in_specs=[pl.BlockSpec((rows, n), lambda i, s: (0, 0)) for _ in pieces]
        + [pl.BlockSpec(memory_space=pl.ANY) for _ in more],
        out_specs=pl.BlockSpec((rows, n), lambda i, s: (0, s[1] ^ (i + first))),
    )
    return pl.pallas_call(
        functools.partial(place_kernel, len(pieces)),
        grid_spec=grid_spec,
        out_shape=jax.ShapeDtypeStruct((rows, n * parts), pieces[0].dtype),
        input_output_aliases={1 + len(pieces): 0} if more else {},
        compiler_params=params(),
    )(scalars, *pieces, *more)


def chip_cycle(chips):
    return list(range(0, chips, 2)) + list(range(chips - 1 - chips % 2, 0, -2))


def ring_gather(shard, chips):
    order = chip_cycle(chips)

    def pairs(step):
        return [
            (2 * order[i] + c, 2 * order[(i + step) % chips] + c)
            for i in range(chips)
            for c in range(2)
        ]

    forth, back = pairs(1), pairs(-1)
    found = [shard]
    a = b = shard
    for hop in range(chips // 2):
        a = lax.ppermute(a, CTX, forth)
        found.append(a)
        if hop < (chips - 1) // 2:
            b = lax.ppermute(b, CTX, back)
            found.append(b)
    return found


def ring_sources(chip, chips):
    order = jnp.array(chip_cycle(chips), jnp.int32)
    place = jnp.sum(jnp.where(order == chip, jnp.arange(chips, dtype=jnp.int32), 0))
    steps = [0]
    for hop in range(chips // 2):
        steps.append(-(hop + 1))
        if hop < (chips - 1) // 2:
            steps.append(hop + 1)
    return order[(place + jnp.array(steps, jnp.int32)) % chips]


def layer(hidden, dest, doc_ids, w_query, key_weight, value_weight):
    rows = hidden.shape[0]
    dp = lax.axis_size(DP)
    size = lax.axis_size(CTX)
    chips = size // 2
    cap = 2 * rows // size
    index = lax.axis_index(CTX)
    chip = index // 2
    core = index % 2
    part = (lax.axis_index(DP) % 2) * 2 + core
    parts = 4
    kq = w_query.shape[1] // parts
    kk = key_weight.shape[1] // parts
    depth = w_query.shape[0]

    core_pairs = [(i, i ^ 1) for i in range(size)]
    side_pairs = [(i, i ^ 1) for i in range(dp)]
    same_core = [[2 * i + c for i in range(chips)] for c in range(2)]

    def to_core(x):
        return lax.ppermute(x, CTX, core_pairs)

    def to_side(x):
        return lax.ppermute(x, DP, side_pairs)

    def exchange(x):
        return lax.all_to_all(
            x, CTX, split_axis=0, concat_axis=0, tiled=True, axis_index_groups=same_core
        )

    ints = to_side(jnp.concatenate([dest, doc_ids]))
    beside = to_side(hidden)

    def columns(g):
        return jnp.concatenate(
            [
                lax.dynamic_slice_in_dim(key_weight, g * kk, kk, 1),
                lax.dynamic_slice_in_dim(value_weight, g * kk, kk, 1),
                lax.dynamic_slice_in_dim(w_query, g * kq, kq, 1),
            ],
            axis=1,
        )

    theirs = columns(part ^ 1)
    theirs = to_core(theirs)
    shard = jnp.concatenate([columns(part), theirs], axis=0)
    ws_kv = ring_gather(shard[:, : 2 * kk], chips)
    ws_q = ring_gather(shard[:, 2 * kk :], chips)
    sources = ring_sources(chip, chips)
    koff = (
        jnp.stack([2 * sources + core, 2 * sources + 1 - core], axis=1).reshape(-1) * depth
    ).astype(jnp.int32)

    across = to_core(hidden)
    diagonal = to_core(beside)
    xs = ((hidden, across), (beside, diagonal))

    both = jnp.stack([dest, ints[:rows]])
    tables = lax.all_to_all(
        jnp.broadcast_to(both[None], (size, 2, rows)),
        CTX,
        split_axis=0,
        concat_axis=0,
        tiled=True,
    )
    tables, _ = lax.optimization_barrier((tables, ws_kv[4]))
    tables = jnp.moveaxis(tables, 1, 0).reshape(2, chips, 2, rows)
    tables = jnp.where(core == 0, tables, tables[:, :, ::-1])
    block = tables // rows
    local = tables % rows
    before = (
        jnp.arange(rows, dtype=jnp.int32)[:, None] < jnp.arange(rows, dtype=jnp.int32)[None, :]
    ).astype(jnp.bfloat16)

    def rank_in(hit):
        return jnp.dot(
            hit.astype(jnp.bfloat16), before, preferred_element_type=jnp.float32
        ).astype(jnp.int32)

    leaving = lax.dynamic_index_in_dim(block, chip, 1, keepdims=False)
    hit = leaving[:, :, None, :] == jnp.arange(size, dtype=jnp.int32)[None, None, :, None]
    rank = jnp.sum(jnp.where(hit, rank_in(hit), 0), axis=2)
    slots = (leaving // 2) * (2 * cap) + ((leaving % 2) ^ core) * cap + rank
    slots = slots.reshape(2, 2, 1, rows)

    mine = 2 * chip + (jnp.arange(2, dtype=jnp.int32) ^ core)
    hit = block[:, None] == mine[None, :, None, None, None]
    rank = rank_in(hit)
    at_slot = hit[..., None, :] & (
        rank[..., None, :] == jnp.arange(cap, dtype=jnp.int32)[:, None]
    )
    targets = jnp.sum(jnp.where(at_slot, local[:, None, :, :, None, :] + 1, 0), axis=-1) - 1
    targets = targets.reshape(2, 2, 1, size * cap)

    half = HEAD // 2
    freq = jnp.arange(half, dtype=jnp.float32)
    inverse = jnp.exp(-(2.0 * freq / HEAD) * jnp.log(jnp.float32(ROPE_BASE)))
    positions = chip * 2 * rows + jnp.arange(2 * rows, dtype=jnp.int32)
    angles = positions.astype(jnp.float32)[:, None] * inverse[None, :]
    cos_half, sin_half = jnp.cos(angles), jnp.sin(angles)
    cosine = jnp.concatenate([cos_half, cos_half], axis=1)
    sine = jnp.concatenate([-sin_half, sin_half], axis=1)
    scalars = jnp.stack([core, part]).astype(jnp.int32)

    def doc_tables(docs):
        padded = jnp.concatenate([jnp.full((rows,), -1, jnp.int32), docs])
        near = lax.dynamic_slice_in_dim(padded, chip * 2 * rows, 3 * rows, 0)
        qdocs = jnp.broadcast_to(near[rows:, None], (2 * rows, HEAD))
        kdocs = jnp.stack([near[: 2 * rows], near[rows:]])[:, None, :]
        return qdocs, kdocs

    docs = (doc_tables(doc_ids), doc_tables(ints[rows:]))
    ahead = [(i, i + 2) for i in range(size - 2)]

    def send(t, ws):
        out = None
        for i, x in enumerate(xs[t]):
            out = project(x, slots[t], ws, koff, 2 * cap, i, out)
        got = exchange(out.reshape(chips, 4 * cap, out.shape[-1]))
        return got.reshape(chips, 2, 2, cap, out.shape[-1])

    def keys_of(t, got):
        first, second = unpack_keys(scalars, got, targets[t], cosine, sine, rows)
        return lax.ppermute(second, CTX, ahead), first, second

    def result(t, d, got, kv3, base=None):
        return attend(d, scalars, got, targets[t], kv3, cosine, sine, *docs[t], base)

    kv_own = keys_of(0, send(0, ws_kv))
    kv_side = keys_of(1, send(1, ws_kv))
    got_side = send(1, ws_q)
    got_own = send(0, ws_q)
    far = result(1, 1, got_side, kv_side)
    far = to_side(far)
    far = to_core(far)
    near = result(1, 0, got_side, kv_side)
    near = to_side(near)
    base = place(scalars, (near, far), 2, parts)
    other = result(0, 1, got_own, kv_own)
    other = to_core(other)
    base = result(0, 0, got_own, kv_own, base)
    return place(scalars, (other,), 1, parts, base)


def solution(mesh):
    placed = (
        P((DP, CTX), None),
        P((DP, CTX)),
        P(DP),
        P(CTX, None),
        P(CTX, None),
        P(CTX, None),
    )
    return jax.shard_map(
        layer, mesh=mesh, in_specs=placed, out_specs=P((DP, CTX), None), check_vma=False
    )
```

```python
import functools

import jax
import jax.numpy as jnp
from jax import lax
from jax.experimental import pallas as pl
from jax.experimental.pallas import tpu as pltpu
from jax.sharding import PartitionSpec as P


HEAD = 128
ROPE_BASE = 500000.0 * 16.0 ** (128.0 / 126.0)
MASKED = -1e30
QT = 128
DP, CTX = "dp", "ctx"


def params(mib=24):
    return pltpu.CompilerParams(vmem_limit_bytes=mib * 1024 * 1024)


def project_kernel(koff, x, slots, *refs):
    *refs, out, y = refs
    i = pl.program_id(0)
    chips, _, per, n = out.shape
    ws = refs[:chips]
    rows = y.shape[0]
    bm = x.shape[0]
    kk = ws[0].shape[0] // 2
    acc = jnp.zeros((bm, n), jnp.float32)
    for k, w in enumerate(ws):
        for h in range(2):
            off = pl.multiple_of(koff[2 * k + h], kk)
            acc = acc + jnp.dot(
                x[:, pl.ds(off, kk)],
                w[h * kk : (h + 1) * kk, :],
                preferred_element_type=jnp.float32,
            )
    y[pl.ds(pl.multiple_of(i * bm, bm), bm), :] = acc.astype(y.dtype)

    @pl.when(i == rows // bm - 1)
    def _():
        step = max(1, 256 // per)
        for a in range(0, chips, step):
            ids = lax.broadcasted_iota(jnp.int32, (step * per, rows), 0) + a * per
            pick = jnp.where(ids == slots[0], 1.0, 0.0).astype(y.dtype)
            part = jnp.dot(pick, y[...], preferred_element_type=jnp.float32)
            out[a : a + step, 0] = part.astype(out.dtype).reshape(step, per, n)


def project(x, slots, ws, koff, per, s, base=None):
    rows, width = x.shape
    n = ws[0].shape[1]
    chips = len(ws)
    bm = rows // 2
    more = [] if base is None else [base]
    grid_spec = pltpu.PrefetchScalarGridSpec(
        num_scalar_prefetch=1,
        grid=(2,),
        in_specs=[
            pl.BlockSpec((bm, width), lambda i, k: (i, 0)),
            pl.BlockSpec((1, 1, rows), lambda i, k: (s, 0, 0)),
        ]
        + [pl.BlockSpec(w.shape, lambda i, k: (0, 0)) for w in ws]
        + [pl.BlockSpec(memory_space=pl.ANY) for _ in more],
        out_specs=pl.BlockSpec((chips, 1, per, n), lambda i, k: (0, s, 0, 0)),
        scratch_shapes=[pltpu.VMEM((rows, n), x.dtype)],
    )
    return pl.pallas_call(
        project_kernel,
        grid_spec=grid_spec,
        out_shape=jax.ShapeDtypeStruct((chips, 2, per, n), x.dtype),
        input_output_aliases={3 + chips: 0} if more else {},
        compiler_params=params(60),
    )(koff, x, slots, *ws, *more)


def unpack_rows(got, target, rows):
    slots = got.shape[0]
    ids = lax.broadcasted_iota(jnp.int32, (rows, slots), 0)
    pick = jnp.where(ids == target, 1.0, 0.0).astype(got.dtype)
    return jnp.dot(pick, got, preferred_element_type=jnp.float32)


def rotated(v, cosine, sine):
    return v * cosine + pltpu.roll(v, HEAD // 2, 1) * sine


def keys_kernel(core, got, target, cosine, sine, first, second):
    v = unpack_rows(got[...].reshape(-1, got.shape[-1]), target[0], first.shape[0])
    k = rotated(v[:, :HEAD], cosine[...], sine[...])
    for e, out in enumerate((first, second)):

        @pl.when(pl.program_id(0) == e)
        def _(out=out):
            out[:, :HEAD] = k.astype(out.dtype)
            out[:, HEAD:] = v[:, HEAD:].astype(out.dtype)


def unpack_keys(core, got, target, cosine, sine, rows):
    chips, _, _, cap, n = got.shape
    grid_spec = pltpu.PrefetchScalarGridSpec(
        num_scalar_prefetch=1,
        grid=(2,),
        in_specs=[
            pl.BlockSpec((chips, 2, 1, cap, n), lambda e, s: (0, 0, e ^ s[0], 0, 0)),
            pl.BlockSpec((1, 1, chips * 2 * cap), lambda e, s: (e ^ s[0], 0, 0)),
            pl.BlockSpec((rows, HEAD), lambda e, s: (e, 0)),
            pl.BlockSpec((rows, HEAD), lambda e, s: (e, 0)),
        ],
        out_specs=[pl.BlockSpec((rows, n), lambda e, s: (0, 0))] * 2,
    )
    return pl.pallas_call(
        keys_kernel,
        grid_spec=grid_spec,
        out_shape=[jax.ShapeDtypeStruct((rows, n), got.dtype)] * 2,
        compiler_params=params(),
    )(core, got, target, cosine, sine)


def attend_kernel(d, core, got, target, *refs):
    *refs, out, q, kv = refs
    *blocks, cosine, sine, qdocs, kdocs = refs[:7]
    rows = out.shape[0]
    heads = got.shape[-1] // HEAD
    span = rows + QT
    v = unpack_rows(got[...].reshape(-1, got.shape[-1]), target[0], rows)
    for h in range(heads):
        turned = rotated(v[:, h * HEAD : (h + 1) * HEAD], cosine[...], sine[...])
        q[h] = (turned * HEAD**-0.5).astype(q.dtype)
    for e in range(2):

        @pl.when(d ^ core[0] == e)
        def _(e=e):
            kv[:rows, : 2 * HEAD] = blocks[e][...]
            kv[rows:, : 2 * HEAD] = blocks[e + 1][...]

    kv[:, 2 * HEAD :] = jnp.ones((2 * rows, HEAD), kv.dtype)

    def tile(i, carry):
        at = pl.multiple_of(i * QT, QT)
        qs = q[:, pl.ds(at, QT), :].reshape(heads * QT, HEAD)
        ks = kv[pl.ds(at, span), :HEAD]
        vs = kv[pl.ds(at, span), HEAD:]
        s = lax.dot_general(
            qs, ks, (((1,), (1,)), ((), ())), preferred_element_type=jnp.float32
        ).reshape(heads, QT, span)
        behind = lax.broadcasted_iota(jnp.int32, (QT, span), 1) - lax.broadcasted_iota(
            jnp.int32, (QT, span), 0
        )
        ok = (behind > 0) & (behind <= rows) & (
            qdocs[pl.ds(at, QT), :1] == kdocs[0, :, pl.ds(at, span)]
        )
        s = jnp.where(ok[None], s, MASKED)
        w = jnp.exp(s - jnp.max(s, axis=-1, keepdims=True))
        o = jnp.dot(
            w.astype(kv.dtype).reshape(heads * QT, span), vs, preferred_element_type=jnp.float32
        ).reshape(heads, QT, 2 * HEAD)
        o = o[..., :HEAD] / o[..., HEAD:]
        for h in range(heads):
            out[pl.ds(at, QT), h * HEAD : (h + 1) * HEAD] = o[h].astype(out.dtype)
        return carry

    lax.fori_loop(0, rows // QT, tile, 0, unroll=2)


def attend(d, scalars, got, target, kv3, cosine, sine, qdocs, kdocs, base=None):
    chips, _, _, cap, n = got.shape
    rows = kv3[0].shape[0]
    more = [] if base is None else [base]
    grid_spec = pltpu.PrefetchScalarGridSpec(
        num_scalar_prefetch=1,
        grid=(1,),
        in_specs=[
            pl.BlockSpec((chips, 2, 1, cap, n), lambda i, s: (0, 0, d, 0, 0)),
            pl.BlockSpec((1, 1, chips * 2 * cap), lambda i, s: (d, 0, 0)),
            *[pl.BlockSpec((rows, 2 * HEAD), lambda i, s: (0, 0))] * 3,
            *[pl.BlockSpec((rows, HEAD), lambda i, s: (d ^ s[0], 0))] * 3,
            pl.BlockSpec((1, 1, 2 * rows), lambda i, s: (d ^ s[0], 0, 0)),
            *[pl.BlockSpec(memory_space=pl.ANY) for _ in more],
        ],
        out_specs=pl.BlockSpec((rows, n), lambda i, s: (0, s[1] if more else 0)),
        scratch_shapes=[
            pltpu.VMEM((n // HEAD, rows, HEAD), got.dtype),
            pltpu.VMEM((2 * rows, 3 * HEAD), got.dtype),
        ],
    )
    shape = base.shape if more else (rows, n)
    return pl.pallas_call(
        functools.partial(attend_kernel, d),
        grid_spec=grid_spec,
        out_shape=jax.ShapeDtypeStruct(shape, got.dtype),
        input_output_aliases={10: 0} if more else {},
        compiler_params=params(),
    )(scalars, got, target, *kv3, cosine, sine, qdocs, kdocs, *more)


def place_kernel(count, scalars, *refs):
    out = refs[-1]
    for k in range(count):

        @pl.when(pl.program_id(0) == k)
        def _(piece=refs[k]):
            out[...] = piece[...]


def place(scalars, pieces, first, parts, base=None):
    rows, n = pieces[0].shape
    more = [] if base is None else [base]
    grid_spec = pltpu.PrefetchScalarGridSpec(
        num_scalar_prefetch=1,
        grid=(len(pieces),),
        in_specs=[pl.BlockSpec((rows, n), lambda i, s: (0, 0)) for _ in pieces]
        + [pl.BlockSpec(memory_space=pl.ANY) for _ in more],
        out_specs=pl.BlockSpec((rows, n), lambda i, s: (0, s[1] ^ (i + first))),
    )
    return pl.pallas_call(
        functools.partial(place_kernel, len(pieces)),
        grid_spec=grid_spec,
        out_shape=jax.ShapeDtypeStruct((rows, n * parts), pieces[0].dtype),
        input_output_aliases={1 + len(pieces): 0} if more else {},
        compiler_params=params(),
    )(scalars, *pieces, *more)


def chip_cycle(chips):
    return list(range(0, chips, 2)) + list(range(chips - 1 - chips % 2, 0, -2))


def ring_gather(shard, chips):
    order = chip_cycle(chips)

    def pairs(step):
        return [
            (2 * order[i] + c, 2 * order[(i + step) % chips] + c)
            for i in range(chips)
            for c in range(2)
        ]

    forth, back = pairs(1), pairs(-1)
    found = [shard]
    a = b = shard
    for hop in range(chips // 2):
        a = lax.ppermute(a, CTX, forth)
        found.append(a)
        if hop < (chips - 1) // 2:
            b = lax.ppermute(b, CTX, back)
            found.append(b)
    return found


def ring_sources(chip, chips):
    order = jnp.array(chip_cycle(chips), jnp.int32)
    place = jnp.sum(jnp.where(order == chip, jnp.arange(chips, dtype=jnp.int32), 0))
    steps = [0]
    for hop in range(chips // 2):
        steps.append(-(hop + 1))
        if hop < (chips - 1) // 2:
            steps.append(hop + 1)
    return order[(place + jnp.array(steps, jnp.int32)) % chips]


def layer(hidden, dest, doc_ids, w_query, key_weight, value_weight):
    rows = hidden.shape[0]
    dp = lax.axis_size(DP)
    size = lax.axis_size(CTX)
    chips = size // 2
    cap = 2 * rows // size
    index = lax.axis_index(CTX)
    chip = index // 2
    core = index % 2
    part = (lax.axis_index(DP) % 2) * 2 + core
    parts = 4
    kq = w_query.shape[1] // parts
    kk = key_weight.shape[1] // parts
    depth = w_query.shape[0]

    core_pairs = [(i, i ^ 1) for i in range(size)]
    side_pairs = [(i, i ^ 1) for i in range(dp)]
    same_core = [[2 * i + c for i in range(chips)] for c in range(2)]

    def to_core(x):
        return lax.ppermute(x, CTX, core_pairs)

    def to_side(x):
        return lax.ppermute(x, DP, side_pairs)

    def exchange(x):
        return lax.all_to_all(
            x, CTX, split_axis=0, concat_axis=0, tiled=True, axis_index_groups=same_core
        )

    ints = to_side(jnp.concatenate([dest, doc_ids]))
    beside = to_side(hidden)

    def columns(g):
        return jnp.concatenate(
            [
                lax.dynamic_slice_in_dim(key_weight, g * kk, kk, 1),
                lax.dynamic_slice_in_dim(value_weight, g * kk, kk, 1),
                lax.dynamic_slice_in_dim(w_query, g * kq, kq, 1),
            ],
            axis=1,
        )

    theirs = columns(part ^ 1)
    theirs = to_core(theirs)
    shard = jnp.concatenate([columns(part), theirs], axis=0)
    ws_kv = ring_gather(shard[:, : 2 * kk], chips)
    ws_q = ring_gather(shard[:, 2 * kk :], chips)
    sources = ring_sources(chip, chips)
    koff = (
        jnp.stack([2 * sources + core, 2 * sources + 1 - core], axis=1).reshape(-1) * depth
    ).astype(jnp.int32)

    across = to_core(hidden)
    diagonal = to_core(beside)
    xs = ((hidden, across), (beside, diagonal))

    both = jnp.stack([dest, ints[:rows]])
    tables = lax.all_to_all(
        jnp.broadcast_to(both[None], (size, 2, rows)),
        CTX,
        split_axis=0,
        concat_axis=0,
        tiled=True,
    )
    tables, _ = lax.optimization_barrier((tables, ws_kv[4]))
    tables = jnp.moveaxis(tables, 1, 0).reshape(2, chips, 2, rows)
    tables = jnp.where(core == 0, tables, tables[:, :, ::-1])
    block = tables // rows
    local = tables % rows
    before = (
        jnp.arange(rows, dtype=jnp.int32)[:, None] < jnp.arange(rows, dtype=jnp.int32)[None, :]
    ).astype(jnp.bfloat16)

    def rank_in(hit):
        return jnp.dot(
            hit.astype(jnp.bfloat16), before, preferred_element_type=jnp.float32
        ).astype(jnp.int32)

    leaving = lax.dynamic_index_in_dim(block, chip, 1, keepdims=False)
    hit = leaving[:, :, None, :] == jnp.arange(size, dtype=jnp.int32)[None, None, :, None]
    rank = jnp.sum(jnp.where(hit, rank_in(hit), 0), axis=2)
    slots = (leaving // 2) * (2 * cap) + ((leaving % 2) ^ core) * cap + rank
    slots = slots.reshape(2, 2, 1, rows)

    mine = 2 * chip + (jnp.arange(2, dtype=jnp.int32) ^ core)
    hit = block[:, None] == mine[None, :, None, None, None]
    rank = rank_in(hit)
    at_slot = hit[..., None, :] & (
        rank[..., None, :] == jnp.arange(cap, dtype=jnp.int32)[:, None]
    )
    targets = jnp.sum(jnp.where(at_slot, local[:, None, :, :, None, :] + 1, 0), axis=-1) - 1
    targets = targets.reshape(2, 2, 1, size * cap)

    half = HEAD // 2
    freq = jnp.arange(half, dtype=jnp.float32)
    inverse = jnp.exp(-(2.0 * freq / HEAD) * jnp.log(jnp.float32(ROPE_BASE)))
    positions = chip * 2 * rows + jnp.arange(2 * rows, dtype=jnp.int32)
    angles = positions.astype(jnp.float32)[:, None] * inverse[None, :]
    cos_half, sin_half = jnp.cos(angles), jnp.sin(angles)
    cosine = jnp.concatenate([cos_half, cos_half], axis=1)
    sine = jnp.concatenate([-sin_half, sin_half], axis=1)
    scalars = jnp.stack([core, part]).astype(jnp.int32)

    def doc_tables(docs):
        padded = jnp.concatenate([jnp.full((rows,), -1, jnp.int32), docs])
        near = lax.dynamic_slice_in_dim(padded, chip * 2 * rows, 3 * rows, 0)
        qdocs = jnp.broadcast_to(near[rows:, None], (2 * rows, HEAD))
        kdocs = jnp.stack([near[: 2 * rows], near[rows:]])[:, None, :]
        return qdocs, kdocs

    docs = (doc_tables(doc_ids), doc_tables(ints[rows:]))
    ahead = [(i, i + 2) for i in range(size - 2)]

    def send(t, ws):
        out = None
        for i, x in enumerate(xs[t]):
            out = project(x, slots[t], ws, koff, 2 * cap, i, out)
        got = exchange(out.reshape(chips, 4 * cap, out.shape[-1]))
        return got.reshape(chips, 2, 2, cap, out.shape[-1])

    def keys_of(t, got):
        first, second = unpack_keys(scalars, got, targets[t], cosine, sine, rows)
        return lax.ppermute(second, CTX, ahead), first, second

    def result(t, d, got, kv3, base=None):
        return attend(d, scalars, got, targets[t], kv3, cosine, sine, *docs[t], base)

    kv_own = keys_of(0, send(0, ws_kv))
    kv_side = keys_of(1, send(1, ws_kv))
    got_side = send(1, ws_q)
    got_own = send(0, ws_q)
    far = result(1, 1, got_side, kv_side)
    far = to_side(far)
    far = to_core(far)
    near = result(1, 0, got_side, kv_side)
    near = to_side(near)
    base = place(scalars, (near, far), 2, parts)
    other = result(0, 1, got_own, kv_own)
    other = to_core(other)
    base = result(0, 0, got_own, kv_own, base)
    return place(scalars, (other,), 1, parts, base)


def solution(mesh):
    placed = (
        P((DP, CTX), None),
        P((DP, CTX)),
        P(DP),
        P(CTX, None),
        P(CTX, None),
        P(CTX, None),
    )
    return jax.shard_map(
        layer, mesh=mesh, in_specs=placed, out_specs=P((DP, CTX), None), check_vma=False
    )
```
